256 devices in a mesh: dp: 4 (over y), space: 64 (over x, z, core).
Axes of the slice: x: 4, y: 4, z: 8, core: 2. Of those that a mesh axis runs over, the one named last changes fastest.
Arguments:
- volume: bfloat16 [4, 128, 4, 64, 128], P('dp', 'space'), may hold values from -30 to 30
- weights_one: bfloat16 [3, 3, 3, 128, 256], replicated, may hold values from -0.109375 to 0.109375
- gain_one: float32 [256], replicated, may hold values from 0.1 to 1.9
- shift_one: float32 [256], replicated, may hold values from -3 to 3
- weights_two: bfloat16 [3, 3, 3, 8, 256], P(None, None, None, None, 'space'), may hold values from -0.4375 to 0.4375
- gain_two: float32 [256], P('space'), may hold values from 0.1 to 1.9
- shift_two: float32 [256], P('space'), may hold values from -3 to 3
- upstream: bfloat16 [4, 256, 64, 2, 32], P('dp', 'space'), may hold values from -6 to 6
Outputs:
- result: bfloat16 [4, 256, 64, 2, 32], P('dp', 'space')
- grad_weights_one: float32 [3, 3, 3, 128, 256], P(None, None, None, None, 'space')
- grad_weights_two: float32 [3, 3, 3, 8, 256], P(None, None, None, None, 'space')
The draws below stay inside these ranges and needn't reach their ends.
All inputs are finite; a program needn't handle non-finite values.
Results may differ from the reference program's by a relative error of at most 0.0057.
Values may be sent and summed in bfloat16 or wider, within the bound.
A program may use at most 64 MiB of HBM per device.

```python
import math
import jax
import jax.numpy as jnp
from jax import lax

C0 = 128
C1 = 256
GROUPS = 32
HI = 4
WI = 64
GSIZE = 8
SAMPLES = 4
DI = 128
DO = 64
HO = 2
WO = 32


def draw_volume(key, part):
    noise_key = jax.random.fold_in(key, 0)
    offset_key = jax.random.fold_in(key, 1)
    common_key = jax.random.fold_in(key, 3)
    phase_key = jax.random.fold_in(key, 4)
    height_key = jax.random.fold_in(key, 5)
    depth = jnp.arange(DI, dtype=jnp.float32) / float(max(DI - 1, 1))
    sample = jnp.arange(SAMPLES, dtype=jnp.float32) / float(max(SAMPLES - 1, 1))
    scale = (1.0 + 2.0 * depth)[None, :, None, None, None] * (1.0 + 2.0 * sample)[:, None, None, None, None]
    offset = 0.3 * jax.random.normal(offset_key, (SAMPLES, DI, 1, 1, C0), jnp.float32)
    loading = jnp.clip(jax.random.normal(common_key, (C0,), jnp.float32), -2.5, 2.5)
    phase = jax.random.uniform(phase_key, (SAMPLES, DI, 1, 1), jnp.float32, 0.0, 2.0 * math.pi)
    height = jax.random.uniform(height_key, (SAMPLES, DI, 1, 1), jnp.float32, 0.7, 1.3)
    rows = jnp.arange(HI, dtype=jnp.float32)[None, None, :, None]
    cols = jnp.arange(WI, dtype=jnp.float32)[None, None, None, :]
    wave = 1.4142 * height * jnp.cos((cols + 3.0 * rows) * (2.0 * math.pi / 32.0) + phase)
    common = 0.6 * wave[..., None] * loading
    noise = jax.random.normal(noise_key, (SAMPLES, DI, HI, WI, C0), jnp.float32)
    values = (0.8 * noise + common) * scale + offset
    return jnp.clip(values, -30.0, 30.0).astype(jnp.bfloat16)


def steps_of(stream_key, extent, shards, smallest, top_value):
    loudness = 1.0
    for position, shards_of in shards:
        heights = jax.random.uniform(jax.random.fold_in(jax.random.fold_in(stream_key, 6), position), (shards_of,), jnp.float32, smallest / len(shards), top_value / len(shards))
        loudness = loudness * jnp.repeat(jnp.exp(heights), extent[position] // shards_of).reshape((-1,) + (1,) * (len(extent) - 1 - position))
    return loudness


def bell_draw(own_key, dims, deviation, most, cuts=(), kind=jnp.bfloat16):
    factor_of = steps_of(own_key, dims, cuts, -0.22, 0.18) if cuts else 1.0
    values = jax.random.normal(own_key, dims, jnp.float32) * deviation * factor_of
    return jnp.minimum(jnp.maximum(values, -most), most).astype(kind)


def setup_inputs(seed: int = 0) -> dict:
    streams_of = jax.random.split(jax.random.key(seed), 9)
    volume = draw_volume(jax.random.fold_in(streams_of[8], 71), 0)
    weights_one = bell_draw(streams_of[1], (3, 3, 3, C0, C1), (27 * C0) ** -0.5, 0.109375)
    gain_one = jnp.clip(1.0 + 0.18 * jax.random.normal(streams_of[2], (C1,), jnp.float32), 0.1, 1.9)
    shift_one = bell_draw(streams_of[3], (C1,), 0.5, 3.0, (), jnp.float32)
    weights_two = bell_draw(streams_of[4], (3, 3, 3, GSIZE, C1), (27 * GSIZE) ** -0.5, 0.4375, ((4, 64),))
    gain_two = jnp.clip(1.0 + 0.18 * jax.random.normal(streams_of[5], (C1,), jnp.float32), 0.1, 1.9)
    shift_two = bell_draw(streams_of[6], (C1,), 0.5, 3.0, ((0, 64),), jnp.float32)
    upstream = bell_draw(streams_of[7], (SAMPLES, C1, DO, HO, WO), 1.0, 6.0, ((0, 4), (1, 64)))
    return {"volume": volume, "weights_one": weights_one, "gain_one": gain_one, "shift_one": shift_one, "weights_two": weights_two, "gain_two": gain_two, "shift_two": shift_two, "upstream": upstream}


EPS = 1e-05
LAST = ('NDHWC', 'DHWIO', 'NDHWC')
FIRST = ('NCDHW', 'DHWIO', 'NCDHW')

def strided_conv(sample, weights):
    return lax.conv_general_dilated(sample[None], weights, (2, 2, 2), ((1, 1), (1, 1), (1, 1)), dimension_numbers=LAST, precision=lax.Precision.HIGHEST)[0]

def grouped_conv(inputs, weights):
    return lax.conv_general_dilated(inputs, weights, (1, 1, 1), ((1, 1), (1, 1), (1, 1)), dimension_numbers=FIRST, feature_group_count=GROUPS, precision=lax.Precision.HIGHEST)

def reference(volume, weights_one, gain_one, shift_one, weights_two, gain_two, shift_two, upstream):
    wide_one = weights_one.astype(jnp.float32)
    pre_one = lax.map(lambda sample: strided_conv(sample.astype(jnp.float32), wide_one), volume)
    count = float(SAMPLES * DO * HO * WO)
    axes_last = (0, 1, 2, 3)
    mean_one = lax.optimization_barrier(jnp.mean(pre_one, axis=axes_last))
    var_one = lax.optimization_barrier(jnp.mean(jnp.square(pre_one - mean_one), axis=axes_last))
    inv_one = lax.rsqrt(var_one + EPS)
    norm_one = (pre_one - mean_one) * inv_one
    act_in = norm_one * gain_one + shift_one
    activated = jax.nn.silu(act_in).astype(jnp.bfloat16)
    act_first = jnp.transpose(activated, (0, 4, 1, 2, 3)).astype(jnp.float32)
    pre_two, pull_two = jax.vjp(grouped_conv, act_first, weights_two.astype(jnp.float32))
    axes_first = (0, 2, 3, 4)
    mean_two = lax.optimization_barrier(jnp.mean(pre_two, axis=axes_first, keepdims=True))
    var_two = lax.optimization_barrier(jnp.mean(jnp.square(pre_two - mean_two), axis=axes_first, keepdims=True))
    inv_two = lax.rsqrt(var_two + EPS)
    norm_two = (pre_two - mean_two) * inv_two
    gain_col = gain_two.reshape((1, -1, 1, 1, 1))
    shift_col = shift_two.reshape((1, -1, 1, 1, 1))
    result = (norm_two * gain_col + shift_col).astype(jnp.bfloat16)
    grad_norm_two = upstream.astype(jnp.float32) * gain_col * (1.0 / math.sqrt(count))
    first_sum = lax.optimization_barrier(jnp.sum(grad_norm_two, axis=axes_first, keepdims=True))
    second_sum = lax.optimization_barrier(jnp.sum(grad_norm_two * norm_two, axis=axes_first, keepdims=True))
    grad_pre_two = (inv_two * (grad_norm_two - first_sum / count - norm_two * (second_sum / count))).astype(jnp.bfloat16)
    grad_first, grad_weights_two = pull_two(grad_pre_two.astype(jnp.float32))
    grad_last = jnp.transpose(grad_first, (0, 2, 3, 4, 1))
    sigma = jax.nn.sigmoid(act_in)
    grad_norm_one = grad_last * (sigma * (1.0 + act_in * (1.0 - sigma))) * gain_one
    third_sum = lax.optimization_barrier(jnp.sum(grad_norm_one, axis=axes_last))
    fourth_sum = lax.optimization_barrier(jnp.sum(grad_norm_one * norm_one, axis=axes_last))
    grad_pre_one = (inv_one * (grad_norm_one - third_sum / count - norm_one * (fourth_sum / count))).astype(jnp.bfloat16)

    def sample_grad(pair):
        sample, cotangent = pair
        wide_sample = sample.astype(jnp.float32)
        unused, pull_one = jax.vjp(lambda weights: strided_conv(wide_sample, weights), wide_one)
        return pull_one(cotangent.astype(jnp.float32))[0]
    grad_weights_one = lax.optimization_barrier(jnp.sum(lax.map(sample_grad, (volume, grad_pre_one)), axis=0))
    return (result, grad_weights_one, grad_weights_two)
```

```python
import math

import jax
import jax.numpy as jnp
from jax import lax
from jax.sharding import PartitionSpec as P

EPS = 1e-05
LAST = ("NDHWC", "DHWIO", "NDHWC")
FIRST = ("NCDHW", "DHWIO", "NCDHW")


def from_behind(value, axis, steps):
    count = lax.axis_size(axis)
    leading, last = (max(0, -steps), min(count, count - steps))
    return lax.ppermute(value, axis, [(source, source + steps) for source in range(leading, last)])


def bits_of(axes):
    size = 1
    for axis in axes:
        size *= lax.axis_size(axis)
    nbits = size.bit_length() - 1
    assert 1 << nbits == size
    return size, nbits


def swap(value, axes, bit, size):
    return lax.ppermute(value, axes, [(d, d ^ (1 << bit)) for d in range(size)])


def butterfly_sum(value, axes):
    size, nbits = bits_of(axes)
    for bit in range(nbits):
        value = value + swap(value, axes, bit, size)
    return value


def butterfly_stats(mean, spread, count, axes):
    size, nbits = bits_of(axes)
    for bit in range(nbits):
        other = swap(jnp.stack([mean, spread]), axes, bit, size)
        other_mean, other_spread = other[0], other[1]
        delta = mean - other_mean
        spread = (spread + other_spread) + delta * delta * (count * 0.5)
        mean = (mean + other_mean) * 0.5
        count = count * 2.0
    return mean, spread, count


def halving_scatter(rows, axis):
    size, nbits = bits_of((axis,))
    index = lax.axis_index(axis)
    tail = rows.shape[1:]
    for bit in range(nbits):
        held = rows.shape[0]
        pairs = rows.reshape((held // 2, 2) + tail)
        mine = (index >> bit) & 1
        keep = lax.dynamic_index_in_dim(pairs, mine, 1, False)
        send = lax.dynamic_index_in_dim(pairs, 1 - mine, 1, False)
        rows = keep + swap(send, axis, bit, size)
    return rows[0]


def group_filter(inputs, grads):
    return lax.conv_general_dilated(
        inputs,
        grads,
        (1, 1, 1),
        ((1, 1), (1, 1), (1, 1)),
        dimension_numbers=("CNDHW", "IODHW", "DHWNC"),
        preferred_element_type=jnp.float32,
    )


def per_device(
    volume, weights_one, gain_one, shift_one, weights_two, gain_two, shift_two, upstream
):
    planes = lax.axis_size("space")
    both = ("dp", "space")
    below = from_behind(volume[:, 1:], "space", 1)
    stacked = jnp.concatenate([below, volume], axis=1)
    pre_one = lax.conv_general_dilated(
        stacked,
        weights_one,
        (2, 2, 2),
        ((0, 0), (1, 1), (1, 1)),
        dimension_numbers=LAST,
        preferred_element_type=jnp.float32,
    )
    lead = pre_one.shape[0]
    local_count_one = float(lead * pre_one.shape[1] * pre_one.shape[2] * pre_one.shape[3])
    count = float(lax.axis_size("dp") * planes) * local_count_one
    axes_last = (0, 1, 2, 3)
    local_mean_one = jnp.mean(pre_one, axis=axes_last)
    local_spread_one = jnp.sum(jnp.square(pre_one - local_mean_one), axis=axes_last)
    mean_one, spread_one, _ = butterfly_stats(local_mean_one, local_spread_one, local_count_one, both)
    var_one = spread_one / count
    inv_one = lax.rsqrt(var_one + EPS)
    norm_one = (pre_one - mean_one) * inv_one
    act_in = norm_one * gain_one + shift_one
    activated = jax.nn.silu(act_in).astype(jnp.bfloat16)
    act_first = jnp.transpose(activated, (0, 4, 1, 2, 3))
    own_width = weights_two.shape[4]
    group_width = weights_two.shape[3]
    window = max(own_width, group_width)
    replicas = window // own_width
    channels = act_first.shape[1]
    tail = act_first.shape[2:]
    parts = act_first.reshape((lead, channels // window, 1, window) + tail)
    copies = jnp.broadcast_to(parts, (lead, channels // window, replicas, window) + tail)
    outgoing = copies.reshape((lead, planes * window) + tail)
    inputs = lax.all_to_all(outgoing, "space", split_axis=1, concat_axis=2, tiled=True)
    groups_here = window // group_width
    per_group = own_width // groups_here
    padding_one = ((1, 1), (1, 1), (1, 1))
    pre_two = lax.conv_general_dilated(
        inputs,
        weights_two,
        (1, 1, 1),
        padding_one,
        dimension_numbers=FIRST,
        feature_group_count=groups_here,
        preferred_element_type=jnp.float32,
    )
    axes_first = (0, 2, 3, 4)
    local_mean_two = jnp.mean(pre_two, axis=axes_first, keepdims=True)
    local_spread_two = jnp.sum(jnp.square(pre_two - local_mean_two), axis=axes_first, keepdims=True)
    local_count_two = float(pre_two.size // pre_two.shape[1])
    mean_two, spread_two, merged_two = butterfly_stats(
        local_mean_two, local_spread_two, local_count_two, ("dp",)
    )
    inv_two = lax.rsqrt(spread_two / merged_two + EPS)
    norm_two = (pre_two - mean_two) * inv_two
    gain_col = gain_two.reshape((1, -1, 1, 1, 1))
    shift_col = shift_two.reshape((1, -1, 1, 1, 1))
    result = (norm_two * gain_col + shift_col).astype(jnp.bfloat16)
    grad_norm_two = upstream.astype(jnp.float32) * gain_col * (1.0 / math.sqrt(count))
    first_sum, second_sum = _pair_sum(
        jnp.sum(grad_norm_two, axis=axes_first, keepdims=True),
        jnp.sum(grad_norm_two * norm_two, axis=axes_first, keepdims=True),
        ("dp",),
    )
    grad_pre_two = (
        inv_two * (grad_norm_two - first_sum / count - norm_two * (second_sum / count))
    ).astype(jnp.bfloat16)
    grouped_inputs = inputs.reshape((lead, groups_here, group_width) + inputs.shape[2:])
    grouped_grads = grad_pre_two.reshape((lead, groups_here, per_group) + grad_pre_two.shape[2:])
    pieces = jax.vmap(group_filter, in_axes=(1, 1))(grouped_inputs, grouped_grads)
    local_two = jnp.transpose(pieces, (1, 2, 3, 4, 0, 5)).reshape((3, 3, 3, group_width, own_width))
    flipped = weights_two[::-1, ::-1, ::-1]
    turned = (
        flipped.reshape((3, 3, 3, group_width, groups_here, per_group))
        .transpose((0, 1, 2, 5, 4, 3))
        .reshape((3, 3, 3, per_group, window))
    )
    partial_grad = lax.conv_general_dilated(
        grad_pre_two,
        turned,
        (1, 1, 1),
        padding_one,
        dimension_numbers=FIRST,
        feature_group_count=groups_here,
        preferred_element_type=jnp.float32,
    )
    arrived = lax.all_to_all(partial_grad, "space", split_axis=2, concat_axis=1, tiled=True)
    grad_act = jnp.sum(
        arrived.reshape((lead, channels // window, replicas, window) + arrived.shape[2:]), axis=2
    ).reshape((lead, channels) + arrived.shape[2:])
    grad_last = jnp.transpose(grad_act, (0, 2, 3, 4, 1))
    sigma = jax.nn.sigmoid(act_in)
    grad_norm_one = grad_last * (sigma * (1.0 + act_in * (1.0 - sigma))) * gain_one
    third_sum, fourth_sum = _pair_sum(
        jnp.sum(grad_norm_one, axis=axes_last),
        jnp.sum(grad_norm_one * norm_one, axis=axes_last),
        both,
    )
    grad_pre_one = (
        inv_one * (grad_norm_one - third_sum / count - norm_one * (fourth_sum / count))
    ).astype(jnp.bfloat16)
    local_one = lax.conv_general_dilated(
        stacked,
        grad_pre_one,
        (1, 1, 1),
        ((0, 0), (1, 0), (1, 0)),
        rhs_dilation=(2, 2, 2),
        dimension_numbers=("CDHWN", "IDHWO", "CDHWN"),
        preferred_element_type=jnp.float32,
    )
    out_channels = local_one.shape[0]
    width = out_channels // planes
    flat = local_one.reshape((planes, -1, 128))
    chunk = halving_scatter(flat, "space")
    chunk_shape = (width,) + local_one.shape[1:]
    joined = jnp.concatenate([chunk.reshape(-1), local_two.reshape(-1)])
    summed = butterfly_sum(joined, ("dp",))
    split = chunk.size
    grad_weights_one = jnp.transpose(summed[:split].reshape(chunk_shape), (1, 2, 3, 4, 0))
    grad_weights_two = summed[split:].reshape(local_two.shape)
    return (result, grad_weights_one, grad_weights_two)


def _pair_sum(first, second, axes):
    stacked = butterfly_sum(jnp.stack([first, second]), axes)
    return stacked[0], stacked[1]


def solution(mesh):
    return jax.shard_map(
        per_device,
        mesh=mesh,
        in_specs=(
            P("dp", "space", None, None, None),
            P(),
            P(),
            P(),
            P(None, None, None, None, "space"),
            P("space"),
            P("space"),
            P("dp", "space", None, None, None),
        ),
        out_specs=(
            P("dp", "space", None, None, None),
            P(None, None, None, None, "space"),
            P(None, None, None, None, "space"),
        ),
        check_vma=False,
    )
```

```python
import math

import jax
import jax.numpy as jnp
from jax import lax
from jax.sharding import PartitionSpec as P

EPS = 1e-05
LAST = ("NDHWC", "DHWIO", "NDHWC")
FIRST = ("NCDHW", "DHWIO", "NCDHW")


def from_behind(value, axis, steps):
    count = lax.axis_size(axis)
    leading, last = (max(0, -steps), min(count, count - steps))
    return lax.ppermute(value, axis, [(source, source + steps) for source in range(leading, last)])


def bits_of(axes):
    size = 1
    for axis in axes:
        size *= lax.axis_size(axis)
    nbits = size.bit_length() - 1
    assert 1 << nbits == size
    return size, nbits


def swap(value, axes, bit, size):
    return lax.ppermute(value, axes, [(d, d ^ (1 << bit)) for d in range(size)])


def butterfly_sum(value, axes):
    size, nbits = bits_of(axes)
    for bit in range(nbits):
        value = value + swap(value, axes, bit, size)
    return value


def butterfly_stats(mean, spread, count, axes):
    size, nbits = bits_of(axes)
    for bit in range(nbits):
        other = swap(jnp.stack([mean, spread]), axes, bit, size)
        other_mean, other_spread = other[0], other[1]
        delta = mean - other_mean
        spread = (spread + other_spread) + delta * delta * (count * 0.5)
        mean = (mean + other_mean) * 0.5
        count = count * 2.0
    return mean, spread, count


def halving_scatter(rows, axis, order, first):
    size, _ = bits_of((axis,))
    index = lax.axis_index(axis)
    tail = rows.shape[1:]
    remaining = list(range(first, first + rows.shape[0].bit_length() - 1))
    for bit in order:
        place = remaining.index(bit)
        held = rows.shape[0]
        view = rows.reshape((held >> (place + 1), 2, 1 << place) + tail)
        mine = (index >> bit) & 1
        keep = lax.dynamic_index_in_dim(view, mine, 1, False)
        send = lax.dynamic_index_in_dim(view, 1 - mine, 1, False)
        rows = (keep + swap(send, axis, bit, size)).reshape((held // 2,) + tail)
        remaining.pop(place)
    return rows[0]


def doubling_gather(value, axis, nbits):
    size, _ = bits_of((axis,))
    index = lax.axis_index(axis)
    held = value[None]
    for bit in range(nbits):
        other = swap(held, axis, bit, size)
        low = ((index >> bit) & 1) == 0
        held = jnp.concatenate([jnp.where(low, held, other), jnp.where(low, other, held)])
    return held


def group_filter(inputs, grads):
    return lax.conv_general_dilated(
        inputs,
        grads,
        (1, 1, 1),
        ((1, 1), (1, 1), (1, 1)),
        dimension_numbers=("CNDHW", "IODHW", "DHWNC"),
        preferred_element_type=jnp.float32,
    )


def per_device(
    volume, weights_one, gain_one, shift_one, weights_two, gain_two, shift_two, upstream
):
    planes = lax.axis_size("space")
    both = ("dp", "space")
    below = from_behind(volume[:, 1:], "space", 1)
    stacked = jnp.concatenate([below, volume], axis=1)
    pre_one = lax.conv_general_dilated(
        stacked,
        weights_one,
        (2, 2, 2),
        ((0, 0), (1, 1), (1, 1)),
        dimension_numbers=LAST,
        preferred_element_type=jnp.float32,
    )
    lead = pre_one.shape[0]
    local_count_one = float(lead * pre_one.shape[1] * pre_one.shape[2] * pre_one.shape[3])
    count = float(lax.axis_size("dp") * planes) * local_count_one
    axes_last = (0, 1, 2, 3)
    local_mean_one = jnp.mean(pre_one, axis=axes_last)
    local_spread_one = jnp.sum(jnp.square(pre_one - local_mean_one), axis=axes_last)
    mean_one, spread_one, _ = butterfly_stats(local_mean_one, local_spread_one, local_count_one, both)
    var_one = spread_one / count
    inv_one = lax.rsqrt(var_one + EPS)
    norm_one = (pre_one - mean_one) * inv_one
    act_in = norm_one * gain_one + shift_one
    activated = jax.nn.silu(act_in).astype(jnp.bfloat16)
    act_first = jnp.transpose(activated, (0, 4, 1, 2, 3))
    own_width = weights_two.shape[4]
    group_width = weights_two.shape[3]
    window = max(own_width, group_width)
    replicas = window // own_width
    channels = act_first.shape[1]
    tail = act_first.shape[2:]
    parts = act_first.reshape((lead, channels // window, 1, window) + tail)
    copies = jnp.broadcast_to(parts, (lead, channels // window, replicas, window) + tail)
    outgoing = copies.reshape((lead, planes * window) + tail)
    inputs = lax.all_to_all(outgoing, "space", split_axis=1, concat_axis=2, tiled=True)
    groups_here = window // group_width
    per_group = own_width // groups_here
    padding_one = ((1, 1), (1, 1), (1, 1))
    pre_two = lax.conv_general_dilated(
        inputs,
        weights_two,
        (1, 1, 1),
        padding_one,
        dimension_numbers=FIRST,
        feature_group_count=groups_here,
        preferred_element_type=jnp.float32,
    )
    axes_first = (0, 2, 3, 4)
    local_mean_two = jnp.mean(pre_two, axis=axes_first, keepdims=True)
    local_spread_two = jnp.sum(jnp.square(pre_two - local_mean_two), axis=axes_first, keepdims=True)
    local_count_two = float(pre_two.size // pre_two.shape[1])
    mean_two, spread_two, merged_two = butterfly_stats(
        local_mean_two, local_spread_two, local_count_two, ("dp",)
    )
    inv_two = lax.rsqrt(spread_two / merged_two + EPS)
    norm_two = (pre_two - mean_two) * inv_two
    gain_col = gain_two.reshape((1, -1, 1, 1, 1))
    shift_col = shift_two.reshape((1, -1, 1, 1, 1))
    result = (norm_two * gain_col + shift_col).astype(jnp.bfloat16)
    grad_norm_two = upstream.astype(jnp.float32) * gain_col * (1.0 / math.sqrt(count))
    first_sum, second_sum = _pair_sum(
        jnp.sum(grad_norm_two, axis=axes_first, keepdims=True),
        jnp.sum(grad_norm_two * norm_two, axis=axes_first, keepdims=True),
        ("dp",),
    )
    grad_pre_two = (
        inv_two * (grad_norm_two - first_sum / count - norm_two * (second_sum / count))
    ).astype(jnp.bfloat16)
    grouped_inputs = inputs.reshape((lead, groups_here, group_width) + inputs.shape[2:])
    grouped_grads = grad_pre_two.reshape((lead, groups_here, per_group) + grad_pre_two.shape[2:])
    pieces = jax.vmap(group_filter, in_axes=(1, 1))(grouped_inputs, grouped_grads)
    local_two = jnp.transpose(pieces, (1, 2, 3, 4, 0, 5)).reshape((3, 3, 3, group_width, own_width))
    flipped = weights_two[::-1, ::-1, ::-1]
    turned = (
        flipped.reshape((3, 3, 3, group_width, groups_here, per_group))
        .transpose((0, 1, 2, 5, 4, 3))
        .reshape((3, 3, 3, per_group, window))
    )
    partial_grad = lax.conv_general_dilated(
        grad_pre_two,
        turned,
        (1, 1, 1),
        padding_one,
        dimension_numbers=FIRST,
        feature_group_count=groups_here,
        preferred_element_type=jnp.float32,
    )
    arrived = lax.all_to_all(partial_grad, "space", split_axis=2, concat_axis=1, tiled=True)
    grad_act = jnp.sum(
        arrived.reshape((lead, channels // window, replicas, window) + arrived.shape[2:]), axis=2
    ).reshape((lead, channels) + arrived.shape[2:])
    grad_last = jnp.transpose(grad_act, (0, 2, 3, 4, 1))
    sigma = jax.nn.sigmoid(act_in)
    grad_norm_one = grad_last * (sigma * (1.0 + act_in * (1.0 - sigma))) * gain_one
    third_sum, fourth_sum = _pair_sum(
        jnp.sum(grad_norm_one, axis=axes_last),
        jnp.sum(grad_norm_one * norm_one, axis=axes_last),
        both,
    )
    grad_pre_one = (
        inv_one * (grad_norm_one - third_sum / count - norm_one * (fourth_sum / count))
    ).astype(jnp.bfloat16)
    gather_bits = 2
    group = 1 << gather_bits
    slab_size = stacked.size
    packed = jnp.concatenate([stacked.reshape(-1), grad_pre_one.reshape(-1)])
    every = doubling_gather(packed, "space", gather_bits)
    slabs = every[:, :slab_size].reshape((group,) + stacked.shape[1:])
    combined = jnp.concatenate(
        [slabs[0, :1], slabs[:, 1:].reshape((-1,) + stacked.shape[2:])]
    )[None]
    grads = every[:, slab_size:].reshape((group,) + grad_pre_one.shape[2:])
    out_channels = grads.shape[-1]
    width = out_channels // planes
    rank = lax.axis_index("space") % group
    grads = grads.reshape(grads.shape[:-1] + (planes // group, group, width))
    mine = lax.dynamic_index_in_dim(grads, rank, grads.ndim - 2, False)
    mine = mine.reshape((1,) + grads.shape[:-3] + (out_channels // group,))
    local_one = lax.conv_general_dilated(
        combined,
        mine,
        (1, 1, 1),
        ((0, 0), (1, 0), (1, 0)),
        rhs_dilation=(2, 2, 2),
        dimension_numbers=("CDHWN", "IDHWO", "CDHWN"),
        preferred_element_type=jnp.float32,
    )
    flat = local_one.reshape((planes // group, -1, 128))
    chunk = halving_scatter(flat, "space", (4, 2, 5, 3), gather_bits)
    chunk_shape = (width,) + local_one.shape[1:]
    joined = jnp.concatenate([chunk.reshape(-1), local_two.reshape(-1)])
    summed = butterfly_sum(joined, ("dp",))
    split = chunk.size
    grad_weights_one = jnp.transpose(summed[:split].reshape(chunk_shape), (1, 2, 3, 4, 0))
    grad_weights_two = summed[split:].reshape(local_two.shape)
    return (result, grad_weights_one, grad_weights_two)


def _pair_sum(first, second, axes):
    stacked = butterfly_sum(jnp.stack([first, second]), axes)
    return stacked[0], stacked[1]


def solution(mesh):
    return jax.shard_map(
        per_device,
        mesh=mesh,
        in_specs=(
            P("dp", "space", None, None, None),
            P(),
            P(),
            P(),
            P(None, None, None, None, "space"),
            P("space"),
            P("space"),
            P("dp", "space", None, None, None),
        ),
        out_specs=(
            P("dp", "space", None, None, None),
            P(None, None, None, None, "space"),
            P(None, None, None, None, "space"),
        ),
        check_vma=False,
    )
```

```python
import math

import jax
import jax.numpy as jnp
from jax import lax
from jax.sharding import PartitionSpec as P

EPS = 1e-05
LAST = ("NDHWC", "DHWIO", "NDHWC")
FIRST = ("NCDHW", "DHWIO", "NCDHW")


def from_behind(value, axis, steps):
    count = lax.axis_size(axis)
    leading, last = (max(0, -steps), min(count, count - steps))
    return lax.ppermute(value, axis, [(source, source + steps) for source in range(leading, last)])


def bits_of(axes):
    size = 1
    for axis in axes:
        size *= lax.axis_size(axis)
    nbits = size.bit_length() - 1
    assert 1 << nbits == size
    return size, nbits


def swap(value, axes, bit, size):
    return lax.ppermute(value, axes, [(d, d ^ (1 << bit)) for d in range(size)])


def butterfly_sum(value, axes):
    size, nbits = bits_of(axes)
    for bit in range(nbits):
        value = value + swap(value, axes, bit, size)
    return value


def butterfly_stats(mean, spread, count, axes):
    size, nbits = bits_of(axes)
    for bit in range(nbits):
        other = swap(jnp.stack([mean, spread]), axes, bit, size)
        other_mean, other_spread = other[0], other[1]
        delta = mean - other_mean
        spread = (spread + other_spread) + delta * delta * (count * 0.5)
        mean = (mean + other_mean) * 0.5
        count = count * 2.0
    return mean, spread, count


def halving_scatter(rows, axis, order, first):
    size, _ = bits_of((axis,))
    index = lax.axis_index(axis)
    tail = rows.shape[1:]
    remaining = list(range(first, first + rows.shape[0].bit_length() - 1))
    for bit in order:
        place = remaining.index(bit)
        held = rows.shape[0]
        view = rows.reshape((held >> (place + 1), 2, 1 << place) + tail)
        mine = (index >> bit) & 1
        keep = lax.dynamic_index_in_dim(view, mine, 1, False)
        send = lax.dynamic_index_in_dim(view, 1 - mine, 1, False)
        rows = (keep + swap(send, axis, bit, size)).reshape((held // 2,) + tail)
        remaining.pop(place)
    return rows[0]


def doubling_gather(value, axis, nbits):
    size, _ = bits_of((axis,))
    index = lax.axis_index(axis)
    held = value[None]
    for bit in range(nbits):
        other = swap(held, axis, bit, size)
        low = ((index >> bit) & 1) == 0
        held = jnp.concatenate([jnp.where(low, held, other), jnp.where(low, other, held)])
    return held


def per_device(
    volume, weights_one, gain_one, shift_one, weights_two, gain_two, shift_two, upstream
):
    planes = lax.axis_size("space")
    both = ("dp", "space")
    below = from_behind(volume[:, 1:], "space", 1)
    stacked = jnp.concatenate([below, volume], axis=1)
    pre_one = lax.conv_general_dilated(
        stacked,
        weights_one,
        (2, 2, 2),
        ((0, 0), (1, 1), (1, 1)),
        dimension_numbers=LAST,
        preferred_element_type=jnp.float32,
    )
    lead = pre_one.shape[0]
    local_count_one = float(lead * pre_one.shape[1] * pre_one.shape[2] * pre_one.shape[3])
    count = float(lax.axis_size("dp") * planes) * local_count_one
    axes_last = (0, 1, 2, 3)
    local_mean_one = jnp.mean(pre_one, axis=axes_last)
    local_spread_one = jnp.sum(jnp.square(pre_one - local_mean_one), axis=axes_last)
    mean_one, spread_one, _ = butterfly_stats(local_mean_one, local_spread_one, local_count_one, both)
    var_one = spread_one / count
    inv_one = lax.rsqrt(var_one + EPS)
    norm_one = (pre_one - mean_one) * inv_one
    act_in = norm_one * gain_one + shift_one
    activated = jax.nn.silu(act_in).astype(jnp.bfloat16)
    act_first = jnp.transpose(activated, (0, 4, 1, 2, 3))
    own_width = weights_two.shape[4]
    group_width = weights_two.shape[3]
    window = max(own_width, group_width)
    replicas = window // own_width
    channels = act_first.shape[1]
    tail = act_first.shape[2:]
    parts = act_first.reshape((lead, channels // window, 1, window) + tail)
    copies = jnp.broadcast_to(parts, (lead, channels // window, replicas, window) + tail)
    outgoing = copies.reshape((lead, planes * window) + tail)
    inputs = lax.all_to_all(outgoing, "space", split_axis=1, concat_axis=2, tiled=True)
    groups_here = window // group_width
    per_group = own_width // groups_here
    padding_one = ((1, 1), (1, 1), (1, 1))
    pre_two = lax.conv_general_dilated(
        inputs,
        weights_two,
        (1, 1, 1),
        padding_one,
        dimension_numbers=FIRST,
        feature_group_count=groups_here,
        preferred_element_type=jnp.float32,
    )
    axes_first = (0, 2, 3, 4)
    local_mean_two = jnp.mean(pre_two, axis=axes_first, keepdims=True)
    local_spread_two = jnp.sum(jnp.square(pre_two - local_mean_two), axis=axes_first, keepdims=True)
    local_count_two = float(pre_two.size // pre_two.shape[1])
    mean_two, spread_two, merged_two = butterfly_stats(
        local_mean_two, local_spread_two, local_count_two, ("dp",)
    )
    inv_two = lax.rsqrt(spread_two / merged_two + EPS)
    norm_two = (pre_two - mean_two) * inv_two
    gain_col = gain_two.reshape((1, -1, 1, 1, 1))
    shift_col = shift_two.reshape((1, -1, 1, 1, 1))
    result = (norm_two * gain_col + shift_col).astype(jnp.bfloat16)
    grad_norm_two = upstream.astype(jnp.float32) * gain_col * (1.0 / math.sqrt(count))
    first_sum, second_sum = _pair_sum(
        jnp.sum(grad_norm_two, axis=axes_first, keepdims=True),
        jnp.sum(grad_norm_two * norm_two, axis=axes_first, keepdims=True),
        ("dp",),
    )
    grad_pre_two = (
        inv_two * (grad_norm_two - first_sum / count - norm_two * (second_sum / count))
    ).astype(jnp.bfloat16)
    spatial = inputs.shape[2:]
    padded = jnp.pad(inputs, ((0, 0), (0, 0), (1, 1), (1, 1), (1, 1)))
    taps = jnp.stack(
        [
            padded[:, :, kd : kd + spatial[0], kh : kh + spatial[1], kw : kw + spatial[2]]
            for kd in range(3)
            for kh in range(3)
            for kw in range(3)
        ]
    ).reshape((27, lead, groups_here, group_width, -1))
    grouped_grads = grad_pre_two.reshape((lead, groups_here, per_group, -1))
    local_two = jnp.einsum(
        "tbgip,bgcp->tigc", taps, grouped_grads, preferred_element_type=jnp.float32
    ).reshape((3, 3, 3, group_width, own_width))
    flipped = weights_two[::-1, ::-1, ::-1]
    turned = (
        flipped.reshape((3, 3, 3, group_width, groups_here, per_group))
        .transpose((0, 1, 2, 5, 4, 3))
        .reshape((3, 3, 3, per_group, window))
    )
    partial_grad = lax.conv_general_dilated(
        grad_pre_two,
        turned,
        (1, 1, 1),
        padding_one,
        dimension_numbers=FIRST,
        feature_group_count=groups_here,
        preferred_element_type=jnp.float32,
    )
    arrived = lax.all_to_all(partial_grad, "space", split_axis=2, concat_axis=1, tiled=True)
    grad_act = jnp.sum(
        arrived.reshape((lead, channels // window, replicas, window) + arrived.shape[2:]), axis=2
    ).reshape((lead, channels) + arrived.shape[2:])
    grad_last = jnp.transpose(grad_act, (0, 2, 3, 4, 1))
    sigma = jax.nn.sigmoid(act_in)
    grad_norm_one = grad_last * (sigma * (1.0 + act_in * (1.0 - sigma))) * gain_one
    third_sum, fourth_sum = _pair_sum(
        jnp.sum(grad_norm_one, axis=axes_last),
        jnp.sum(grad_norm_one * norm_one, axis=axes_last),
        both,
    )
    grad_pre_one = (
        inv_one * (grad_norm_one - third_sum / count - norm_one * (fourth_sum / count))
    ).astype(jnp.bfloat16)
    gather_bits = 2
    group = 1 << gather_bits
    slab_size = stacked.size
    out_channels = grad_pre_one.shape[-1]
    width = out_channels // planes
    rows_one = grad_pre_one.shape[2:-1]
    ordered = jnp.moveaxis(
        grad_pre_one.reshape(rows_one + (planes // group, group, width)), -2, 0
    )
    packed = jnp.concatenate([stacked.reshape(-1), ordered.reshape(-1)])
    every = doubling_gather(packed, "space", gather_bits)
    slabs = every[:, :slab_size].reshape((group,) + stacked.shape[1:])
    combined = jnp.concatenate(
        [slabs[0, :1], slabs[:, 1:].reshape((-1,) + stacked.shape[2:])]
    )[None]
    grads = every[:, slab_size:].reshape((group, group) + rows_one + (out_channels // group,))
    rank = lax.axis_index("space") % group
    mine = lax.dynamic_index_in_dim(grads, rank, 1, False)[None]
    local_one = lax.conv_general_dilated(
        combined,
        mine,
        (1, 1, 1),
        ((0, 0), (1, 0), (1, 0)),
        rhs_dilation=(2, 2, 2),
        dimension_numbers=("CDHWN", "IDHWO", "CDHWN"),
        preferred_element_type=jnp.float32,
    )
    flat = local_one.reshape((planes // group, -1, 128))
    chunk = halving_scatter(flat, "space", (4, 2, 5, 3), gather_bits)
    chunk_shape = (width,) + local_one.shape[1:]
    joined = jnp.concatenate([chunk.reshape(-1), local_two.reshape(-1)])
    summed = butterfly_sum(joined, ("dp",))
    split = chunk.size
    grad_weights_one = jnp.transpose(summed[:split].reshape(chunk_shape), (1, 2, 3, 4, 0))
    grad_weights_two = summed[split:].reshape(local_two.shape)
    return (result, grad_weights_one, grad_weights_two)


def _pair_sum(first, second, axes):
    stacked = butterfly_sum(jnp.stack([first, second]), axes)
    return stacked[0], stacked[1]


def solution(mesh):
    return jax.shard_map(
        per_device,
        mesh=mesh,
        in_specs=(
            P("dp", "space", None, None, None),
            P(),
            P(),
            P(),
            P(None, None, None, None, "space"),
            P("space"),
            P("space"),
            P("dp", "space", None, None, None),
        ),
        out_specs=(
            P("dp", "space", None, None, None),
            P(None, None, None, None, "space"),
            P(None, None, None, None, "space"),
        ),
        check_vma=False,
    )
```

```python
import math

import jax
import jax.numpy as jnp
from jax import lax
from jax.sharding import PartitionSpec as P

EPS = 1e-05
LAST = ("NDHWC", "DHWIO", "NDHWC")
FIRST = ("NCDHW", "DHWIO", "NCDHW")


def from_behind(value, axis, steps):
    count = lax.axis_size(axis)
    leading, last = (max(0, -steps), min(count, count - steps))
    return lax.ppermute(value, axis, [(source, source + steps) for source in range(leading, last)])


def bits_of(axes):
    size = 1
    for axis in axes:
        size *= lax.axis_size(axis)
    nbits = size.bit_length() - 1
    assert 1 << nbits == size
    return size, nbits


def swap(value, axes, bit, size):
    return lax.ppermute(value, axes, [(d, d ^ (1 << bit)) for d in range(size)])


def butterfly_sum(value, axes):
    size, nbits = bits_of(axes)
    for bit in range(nbits):
        value = value + swap(value, axes, bit, size)
    return value


def butterfly_stats(mean, spread, count, axes):
    size, nbits = bits_of(axes)
    for bit in range(nbits):
        other = swap(jnp.stack([mean, spread]), axes, bit, size)
        other_mean, other_spread = other[0], other[1]
        delta = mean - other_mean
        spread = (spread + other_spread) + delta * delta * (count * 0.5)
        mean = (mean + other_mean) * 0.5
        count = count * 2.0
    return mean, spread, count


def halving_scatter(rows, axis, order, first):
    size, _ = bits_of((axis,))
    index = lax.axis_index(axis)
    tail = rows.shape[1:]
    remaining = list(range(first, first + rows.shape[0].bit_length() - 1))
    for bit in order:
        place = remaining.index(bit)
        held = rows.shape[0]
        view = rows.reshape((held >> (place + 1), 2, 1 << place) + tail)
        mine = (index >> bit) & 1
        keep = lax.dynamic_index_in_dim(view, mine, 1, False)
        send = lax.dynamic_index_in_dim(view, 1 - mine, 1, False)
        rows = (keep + swap(send, axis, bit, size)).reshape((held // 2,) + tail)
        remaining.pop(place)
    return rows[0]


def doubling_gather(value, axis, nbits):
    size, _ = bits_of((axis,))
    index = lax.axis_index(axis)
    held = value[None]
    for bit in range(nbits):
        other = swap(held, axis, bit, size)
        low = ((index >> bit) & 1) == 0
        held = jnp.concatenate([jnp.where(low, held, other), jnp.where(low, other, held)])
    return held


def group_filter(inputs, grads):
    return lax.conv_general_dilated(
        inputs,
        grads,
        (1, 1, 1),
        ((1, 1), (1, 1), (1, 1)),
        dimension_numbers=("CNDHW", "IODHW", "DHWNC"),
        preferred_element_type=jnp.float32,
    )


def per_device(
    volume, weights_one, gain_one, shift_one, weights_two, gain_two, shift_two, upstream
):
    planes = lax.axis_size("space")
    both = ("dp", "space")
    below = from_behind(volume[:, 1:], "space", 1)
    stacked = jnp.concatenate([below, volume], axis=1)
    pre_one = lax.conv_general_dilated(
        stacked,
        weights_one,
        (2, 2, 2),
        ((0, 0), (1, 1), (1, 1)),
        dimension_numbers=LAST,
        preferred_element_type=jnp.float32,
    )
    lead = pre_one.shape[0]
    local_count_one = float(lead * pre_one.shape[1] * pre_one.shape[2] * pre_one.shape[3])
    count = float(lax.axis_size("dp") * planes) * local_count_one
    axes_last = (0, 1, 2, 3)
    local_mean_one = jnp.mean(pre_one, axis=axes_last)
    local_spread_one = jnp.sum(jnp.square(pre_one - local_mean_one), axis=axes_last)
    mean_one, spread_one, _ = butterfly_stats(local_mean_one, local_spread_one, local_count_one, both)
    var_one = spread_one / count
    inv_one = lax.rsqrt(var_one + EPS)
    norm_one = (pre_one - mean_one) * inv_one
    act_in = norm_one * gain_one + shift_one
    activated = jax.nn.silu(act_in).astype(jnp.bfloat16)
    act_first = jnp.transpose(activated, (0, 4, 1, 2, 3))
    own_width = weights_two.shape[4]
    group_width = weights_two.shape[3]
    window = max(own_width, group_width)
    replicas = window // own_width
    channels = act_first.shape[1]
    tail = act_first.shape[2:]
    parts = act_first.reshape((lead, channels // window, 1, window) + tail)
    copies = jnp.broadcast_to(parts, (lead, channels // window, replicas, window) + tail)
    outgoing = copies.reshape((lead, planes * window) + tail)
    inputs = lax.all_to_all(outgoing, "space", split_axis=1, concat_axis=2, tiled=True)
    groups_here = window // group_width
    per_group = own_width // groups_here
    padding_one = ((1, 1), (1, 1), (1, 1))
    pre_two = lax.conv_general_dilated(
        inputs,
        weights_two,
        (1, 1, 1),
        padding_one,
        dimension_numbers=FIRST,
        feature_group_count=groups_here,
        preferred_element_type=jnp.float32,
    )
    axes_first = (0, 2, 3, 4)
    local_mean_two = jnp.mean(pre_two, axis=axes_first, keepdims=True)
    local_spread_two = jnp.sum(jnp.square(pre_two - local_mean_two), axis=axes_first, keepdims=True)
    local_count_two = float(pre_two.size // pre_two.shape[1])
    mean_two, spread_two, merged_two = butterfly_stats(
        local_mean_two, local_spread_two, local_count_two, ("dp",)
    )
    inv_two = lax.rsqrt(spread_two / merged_two + EPS)
    norm_two = (pre_two - mean_two) * inv_two
    gain_col = gain_two.reshape((1, -1, 1, 1, 1))
    shift_col = shift_two.reshape((1, -1, 1, 1, 1))
    result = (norm_two * gain_col + shift_col).astype(jnp.bfloat16)
    grad_norm_two = upstream.astype(jnp.float32) * gain_col * (1.0 / math.sqrt(count))
    first_sum, second_sum = _pair_sum(
        jnp.sum(grad_norm_two, axis=axes_first, keepdims=True),
        jnp.sum(grad_norm_two * norm_two, axis=axes_first, keepdims=True),
        ("dp",),
    )
    grad_pre_two = (
        inv_two * (grad_norm_two - first_sum / count - norm_two * (second_sum / count))
    ).astype(jnp.bfloat16)
    grouped_inputs = inputs.reshape((lead, groups_here, group_width) + inputs.shape[2:])
    grouped_grads = grad_pre_two.reshape((lead, groups_here, per_group) + grad_pre_two.shape[2:])
    pieces = jax.vmap(group_filter, in_axes=(1, 1))(grouped_inputs, grouped_grads)
    local_two = jnp.transpose(pieces, (1, 2, 3, 4, 0, 5)).reshape((3, 3, 3, group_width, own_width))
    flipped = weights_two[::-1, ::-1, ::-1]
    turned = (
        flipped.reshape((3, 3, 3, group_width, groups_here, per_group))
        .transpose((0, 1, 2, 5, 4, 3))
        .reshape((3, 3, 3, per_group, window))
    )
    partial_grad = lax.conv_general_dilated(
        grad_pre_two,
        turned,
        (1, 1, 1),
        padding_one,
        dimension_numbers=FIRST,
        feature_group_count=groups_here,
        preferred_element_type=jnp.float32,
    )
    arrived = lax.all_to_all(partial_grad, "space", split_axis=2, concat_axis=1, tiled=True)
    grad_act = jnp.sum(
        arrived.reshape((lead, channels // window, replicas, window) + arrived.shape[2:]), axis=2
    ).reshape((lead, channels) + arrived.shape[2:])
    grad_last = jnp.transpose(grad_act, (0, 2, 3, 4, 1))
    sigma = jax.nn.sigmoid(act_in)
    grad_norm_one = grad_last * (sigma * (1.0 + act_in * (1.0 - sigma))) * gain_one
    third_sum, fourth_sum = _pair_sum(
        jnp.sum(grad_norm_one, axis=axes_last),
        jnp.sum(grad_norm_one * norm_one, axis=axes_last),
        both,
    )
    grad_pre_one = (
        inv_one * (grad_norm_one - third_sum / count - norm_one * (fourth_sum / count))
    ).astype(jnp.bfloat16)
    gather_bits = 2
    group = 1 << gather_bits
    slab_size = stacked.size
    out_channels = grad_pre_one.shape[-1]
    width = out_channels // planes
    rows_one = grad_pre_one.shape[2:-1]
    ordered = jnp.moveaxis(
        grad_pre_one.reshape(rows_one + (planes // group, group, width)), -2, 0
    )
    packed = jnp.concatenate([stacked.reshape(-1), ordered.reshape(-1)])
    every = doubling_gather(packed, "space", gather_bits)
    slabs = every[:, :slab_size].reshape((group,) + stacked.shape[1:])
    combined = jnp.concatenate(
        [slabs[0, :1], slabs[:, 1:].reshape((-1,) + stacked.shape[2:])]
    )[None]
    grads = every[:, slab_size:].reshape((group, group) + rows_one + (out_channels // group,))
    rank = lax.axis_index("space") % group
    mine = lax.dynamic_index_in_dim(grads, rank, 1, False)[None]
    local_one = lax.conv_general_dilated(
        combined,
        mine,
        (1, 1, 1),
        ((0, 0), (1, 0), (1, 0)),
        rhs_dilation=(2, 2, 2),
        dimension_numbers=("CDHWN", "IDHWO", "CDHWN"),
        preferred_element_type=jnp.float32,
    )
    flat = local_one.reshape((planes // group, -1, 128))
    chunk = halving_scatter(flat, "space", (4, 2, 5, 3), gather_bits)
    chunk_shape = (width,) + local_one.shape[1:]
    joined = jnp.concatenate([chunk.reshape(-1), local_two.reshape(-1)])
    summed = butterfly_sum(joined, ("dp",))
    split = chunk.size
    grad_weights_one = jnp.transpose(summed[:split].reshape(chunk_shape), (1, 2, 3, 4, 0))
    grad_weights_two = summed[split:].reshape(local_two.shape)
    return (result, grad_weights_one, grad_weights_two)


def _pair_sum(first, second, axes):
    stacked = butterfly_sum(jnp.stack([first, second]), axes)
    return stacked[0], stacked[1]


def solution(mesh):
    return jax.shard_map(
        per_device,
        mesh=mesh,
        in_specs=(
            P("dp", "space", None, None, None),
            P(),
            P(),
            P(),
            P(None, None, None, None, "space"),
            P("space"),
            P("space"),
            P("dp", "space", None, None, None),
        ),
        out_specs=(
            P("dp", "space", None, None, None),
            P(None, None, None, None, "space"),
            P(None, None, None, None, "space"),
        ),
        check_vma=False,
    )
```

```python
import math

import jax
import jax.numpy as jnp
from jax import lax
from jax.sharding import PartitionSpec as P

EPS = 1e-05
LAST = ("NDHWC", "DHWIO", "NDHWC")
FIRST = ("NCDHW", "DHWIO", "NCDHW")


def from_behind(value, axis, steps):
    count = lax.axis_size(axis)
    leading, last = (max(0, -steps), min(count, count - steps))
    return lax.ppermute(value, axis, [(source, source + steps) for source in range(leading, last)])


def bits_of(axes):
    size = 1
    for axis in axes:
        size *= lax.axis_size(axis)
    nbits = size.bit_length() - 1
    assert 1 << nbits == size
    return size, nbits


def swap(value, axes, bit, size):
    return lax.ppermute(value, axes, [(d, d ^ (1 << bit)) for d in range(size)])


def butterfly_sum(value, axes):
    size, nbits = bits_of(axes)
    for bit in range(nbits):
        value = value + swap(value, axes, bit, size)
    return value


def butterfly_stats(mean, spread, count, axes):
    size, nbits = bits_of(axes)
    for bit in range(nbits):
        other = swap(jnp.stack([mean, spread]), axes, bit, size)
        other_mean, other_spread = other[0], other[1]
        delta = mean - other_mean
        spread = (spread + other_spread) + delta * delta * (count * 0.5)
        mean = (mean + other_mean) * 0.5
        count = count * 2.0
    return mean, spread, count


def halving_scatter(rows, axis, order, first):
    size, _ = bits_of((axis,))
    index = lax.axis_index(axis)
    tail = rows.shape[1:]
    remaining = list(range(first, first + rows.shape[0].bit_length() - 1))
    for bit in order:
        place = remaining.index(bit)
        held = rows.shape[0]
        view = rows.reshape((held >> (place + 1), 2, 1 << place) + tail)
        mine = (index >> bit) & 1
        keep = lax.dynamic_index_in_dim(view, mine, 1, False)
        send = lax.dynamic_index_in_dim(view, 1 - mine, 1, False)
        rows = (keep + swap(send, axis, bit, size)).reshape((held // 2,) + tail)
        remaining.pop(place)
    return rows[0]


def doubling_gather(value, axis, nbits):
    size, _ = bits_of((axis,))
    index = lax.axis_index(axis)
    held = value[None]
    for bit in range(nbits):
        other = swap(held, axis, bit, size)
        low = ((index >> bit) & 1) == 0
        held = jnp.concatenate([jnp.where(low, held, other), jnp.where(low, other, held)])
    return held


def group_filter(inputs, grads):
    return lax.conv_general_dilated(
        inputs,
        grads,
        (1, 1, 1),
        ((1, 1), (1, 1), (1, 1)),
        dimension_numbers=("CNDHW", "IODHW", "DHWNC"),
        preferred_element_type=jnp.float32,
    )


def per_device(
    volume, weights_one, gain_one, shift_one, weights_two, gain_two, shift_two, upstream
):
    planes = lax.axis_size("space")
    both = ("dp", "space")
    below = from_behind(volume[:, 1:], "space", 1)
    stacked = jnp.concatenate([below, volume], axis=1)
    pre_one = lax.conv_general_dilated(
        stacked,
        weights_one,
        (2, 2, 2),
        ((0, 0), (1, 1), (1, 1)),
        dimension_numbers=LAST,
        preferred_element_type=jnp.float32,
    )
    lead = pre_one.shape[0]
    local_count_one = float(lead * pre_one.shape[1] * pre_one.shape[2] * pre_one.shape[3])
    count = float(lax.axis_size("dp") * planes) * local_count_one
    axes_last = (0, 1, 2, 3)
    local_mean_one = jnp.mean(pre_one, axis=axes_last)
    local_spread_one = jnp.sum(jnp.square(pre_one - local_mean_one), axis=axes_last)
    mean_one, spread_one, _ = butterfly_stats(local_mean_one, local_spread_one, local_count_one, both)
    var_one = spread_one / count
    inv_one = lax.rsqrt(var_one + EPS)
    norm_one = (pre_one - mean_one) * inv_one
    act_in = norm_one * gain_one + shift_one
    activated = jax.nn.silu(act_in).astype(jnp.bfloat16)
    act_first = jnp.transpose(activated, (0, 4, 1, 2, 3))
    own_width = weights_two.shape[4]
    group_width = weights_two.shape[3]
    window = max(own_width, group_width)
    replicas = window // own_width
    channels = act_first.shape[1]
    tail = act_first.shape[2:]
    parts = act_first.reshape((lead, channels // window, 1, window) + tail)
    copies = jnp.broadcast_to(parts, (lead, channels // window, replicas, window) + tail)
    outgoing = copies.reshape((lead, planes * window) + tail)
    inputs = lax.all_to_all(outgoing, "space", split_axis=1, concat_axis=2, tiled=True)
    groups_here = window // group_width
    per_group = own_width // groups_here
    padding_one = ((1, 1), (1, 1), (1, 1))
    pre_two = lax.conv_general_dilated(
        inputs,
        weights_two,
        (1, 1, 1),
        padding_one,
        dimension_numbers=FIRST,
        feature_group_count=groups_here,
        preferred_element_type=jnp.float32,
    )
    axes_first = (0, 2, 3, 4)
    local_mean_two = jnp.mean(pre_two, axis=axes_first, keepdims=True)
    local_spread_two = jnp.sum(jnp.square(pre_two - local_mean_two), axis=axes_first, keepdims=True)
    local_count_two = float(pre_two.size // pre_two.shape[1])
    mean_two, spread_two, merged_two = butterfly_stats(
        local_mean_two, local_spread_two, local_count_two, ("dp",)
    )
    inv_two = lax.rsqrt(spread_two / merged_two + EPS)
    norm_two = (pre_two - mean_two) * inv_two
    gain_col = gain_two.reshape((1, -1, 1, 1, 1))
    shift_col = shift_two.reshape((1, -1, 1, 1, 1))
    result = (norm_two * gain_col + shift_col).astype(jnp.bfloat16)
    grad_norm_two = upstream.astype(jnp.float32) * gain_col * (1.0 / math.sqrt(count))
    first_sum, second_sum = _pair_sum(
        jnp.sum(grad_norm_two, axis=axes_first, keepdims=True),
        jnp.sum(grad_norm_two * norm_two, axis=axes_first, keepdims=True),
        ("dp",),
    )
    grad_pre_two = (
        inv_two * (grad_norm_two - first_sum / count - norm_two * (second_sum / count))
    ).astype(jnp.bfloat16)
    grouped_inputs = inputs.reshape((lead, groups_here, group_width) + inputs.shape[2:])
    grouped_grads = grad_pre_two.reshape((lead, groups_here, per_group) + grad_pre_two.shape[2:])
    pieces = jax.vmap(group_filter, in_axes=(1, 1))(grouped_inputs, grouped_grads)
    local_two = jnp.transpose(pieces, (1, 2, 3, 4, 0, 5)).reshape((3, 3, 3, group_width, own_width))
    grad_weights_two = butterfly_sum(local_two, ("dp",))
    flipped = weights_two[::-1, ::-1, ::-1]
    turned = (
        flipped.reshape((3, 3, 3, group_width, groups_here, per_group))
        .transpose((0, 1, 2, 5, 4, 3))
        .reshape((3, 3, 3, per_group, window))
    )
    partial_grad = lax.conv_general_dilated(
        grad_pre_two,
        turned,
        (1, 1, 1),
        padding_one,
        dimension_numbers=FIRST,
        feature_group_count=groups_here,
        preferred_element_type=jnp.float32,
    )
    arrived = lax.all_to_all(partial_grad, "space", split_axis=2, concat_axis=1, tiled=True)
    grad_act = jnp.sum(
        arrived.reshape((lead, channels // window, replicas, window) + arrived.shape[2:]), axis=2
    ).reshape((lead, channels) + arrived.shape[2:])
    grad_last = jnp.transpose(grad_act, (0, 2, 3, 4, 1))
    sigma = jax.nn.sigmoid(act_in)
    grad_norm_one = grad_last * (sigma * (1.0 + act_in * (1.0 - sigma))) * gain_one
    third_sum, fourth_sum = _pair_sum(
        jnp.sum(grad_norm_one, axis=axes_last),
        jnp.sum(grad_norm_one * norm_one, axis=axes_last),
        both,
    )
    grad_pre_one = (
        inv_one * (grad_norm_one - third_sum / count - norm_one * (fourth_sum / count))
    ).astype(jnp.bfloat16)
    gather_bits = 2
    group = 1 << gather_bits
    slab_size = stacked.size
    out_channels = grad_pre_one.shape[-1]
    width = out_channels // planes
    rows_one = grad_pre_one.shape[2:-1]
    ordered = jnp.moveaxis(
        grad_pre_one.reshape(rows_one + (planes // group, group, width)), -2, 0
    )
    packed = jnp.concatenate([stacked.reshape(-1), ordered.reshape(-1)])
    every = doubling_gather(packed, "space", gather_bits)
    slabs = every[:, :slab_size].reshape((group,) + stacked.shape[1:])
    combined = jnp.concatenate(
        [slabs[0, :1], slabs[:, 1:].reshape((-1,) + stacked.shape[2:])]
    )[None]
    grads = every[:, slab_size:].reshape((group, group) + rows_one + (out_channels // group,))
    rank = lax.axis_index("space") % group
    mine = lax.dynamic_index_in_dim(grads, rank, 1, False)[None]
    local_one = lax.conv_general_dilated(
        combined,
        mine,
        (1, 1, 1),
        ((0, 0), (1, 0), (1, 0)),
        rhs_dilation=(2, 2, 2),
        dimension_numbers=("CDHWN", "IDHWO", "CDHWN"),
        preferred_element_type=jnp.float32,
    )
    flat = local_one.reshape((planes // group, -1, 128))
    chunk = halving_scatter(flat, "space", (4, 2, 5, 3), gather_bits)
    chunk_shape = (width,) + local_one.shape[1:]
    summed = butterfly_sum(chunk, ("dp",))
    grad_weights_one = jnp.transpose(summed.reshape(chunk_shape), (1, 2, 3, 4, 0))
    return (result, grad_weights_one, grad_weights_two)


def _pair_sum(first, second, axes):
    stacked = butterfly_sum(jnp.stack([first, second]), axes)
    return stacked[0], stacked[1]


def solution(mesh):
    return jax.shard_map(
        per_device,
        mesh=mesh,
        in_specs=(
            P("dp", "space", None, None, None),
            P(),
            P(),
            P(),
            P(None, None, None, None, "space"),
            P("space"),
            P("space"),
            P("dp", "space", None, None, None),
        ),
        out_specs=(
            P("dp", "space", None, None, None),
            P(None, None, None, None, "space"),
            P(None, None, None, None, "space"),
        ),
        check_vma=False,
    )
```

```python
import math

import jax
import jax.numpy as jnp
from jax import lax
from jax.sharding import PartitionSpec as P

EPS = 1e-05
LAST = ("NDHWC", "DHWIO", "NDHWC")
FIRST = ("NCDHW", "DHWIO", "NCDHW")


def from_behind(value, axis, steps):
    count = lax.axis_size(axis)
    leading, last = (max(0, -steps), min(count, count - steps))
    return lax.ppermute(value, axis, [(source, source + steps) for source in range(leading, last)])


def bits_of(axes):
    size = 1
    for axis in axes:
        size *= lax.axis_size(axis)
    nbits = size.bit_length() - 1
    assert 1 << nbits == size
    return size, nbits


def swap(value, axes, bit, size):
    return lax.ppermute(value, axes, [(d, d ^ (1 << bit)) for d in range(size)])


def butterfly_sum(value, axes):
    size, nbits = bits_of(axes)
    for bit in range(nbits):
        value = value + swap(value, axes, bit, size)
    return value


def butterfly_stats(mean, spread, count, axes):
    size, nbits = bits_of(axes)
    for bit in range(nbits):
        other = swap(jnp.stack([mean, spread]), axes, bit, size)
        other_mean, other_spread = other[0], other[1]
        delta = mean - other_mean
        spread = (spread + other_spread) + delta * delta * (count * 0.5)
        mean = (mean + other_mean) * 0.5
        count = count * 2.0
    return mean, spread, count


def halving_scatter(parts, axis, orders, first):
    size, _ = bits_of((axis,))
    index = lax.axis_index(axis)
    parts = list(parts)
    remaining = [list(range(first, first + rows.shape[0].bit_length() - 1)) for rows in parts]
    for bits in zip(*orders):
        for which, bit in enumerate(bits):
            rows = parts[which]
            tail = rows.shape[1:]
            place = remaining[which].index(bit)
            held = rows.shape[0]
            view = rows.reshape((held >> (place + 1), 2, 1 << place) + tail)
            mine = (index >> bit) & 1
            keep = lax.dynamic_index_in_dim(view, mine, 1, False)
            send = lax.dynamic_index_in_dim(view, 1 - mine, 1, False)
            parts[which] = (keep + swap(send, axis, bit, size)).reshape((held // 2,) + tail)
            remaining[which].pop(place)
    return [rows[0] for rows in parts]


def doubling_gather(value, axis, nbits):
    size, _ = bits_of((axis,))
    index = lax.axis_index(axis)
    held = value[None]
    for bit in range(nbits):
        other = swap(held, axis, bit, size)
        low = ((index >> bit) & 1) == 0
        held = jnp.concatenate([jnp.where(low, held, other), jnp.where(low, other, held)])
    return held


def group_filter(inputs, grads):
    return lax.conv_general_dilated(
        inputs,
        grads,
        (1, 1, 1),
        ((1, 1), (1, 1), (1, 1)),
        dimension_numbers=("CNDHW", "IODHW", "DHWNC"),
        preferred_element_type=jnp.float32,
    )


def per_device(
    volume, weights_one, gain_one, shift_one, weights_two, gain_two, shift_two, upstream
):
    planes = lax.axis_size("space")
    both = ("dp", "space")
    below = from_behind(volume[:, 1:], "space", 1)
    stacked = jnp.concatenate([below, volume], axis=1)
    pre_one = lax.conv_general_dilated(
        stacked,
        weights_one,
        (2, 2, 2),
        ((0, 0), (1, 1), (1, 1)),
        dimension_numbers=LAST,
        preferred_element_type=jnp.float32,
    )
    lead = pre_one.shape[0]
    local_count_one = float(lead * pre_one.shape[1] * pre_one.shape[2] * pre_one.shape[3])
    count = float(lax.axis_size("dp") * planes) * local_count_one
    axes_last = (0, 1, 2, 3)
    local_mean_one = jnp.mean(pre_one, axis=axes_last)
    local_spread_one = jnp.sum(jnp.square(pre_one - local_mean_one), axis=axes_last)
    mean_one, spread_one, _ = butterfly_stats(local_mean_one, local_spread_one, local_count_one, both)
    var_one = spread_one / count
    inv_one = lax.rsqrt(var_one + EPS)
    norm_one = (pre_one - mean_one) * inv_one
    act_in = norm_one * gain_one + shift_one
    activated = jax.nn.silu(act_in).astype(jnp.bfloat16)
    act_first = jnp.transpose(activated, (0, 4, 1, 2, 3))
    own_width = weights_two.shape[4]
    group_width = weights_two.shape[3]
    window = max(own_width, group_width)
    replicas = window // own_width
    channels = act_first.shape[1]
    tail = act_first.shape[2:]
    parts = act_first.reshape((lead, channels // window, 1, window) + tail)
    copies = jnp.broadcast_to(parts, (lead, channels // window, replicas, window) + tail)
    outgoing = copies.reshape((lead, planes * window) + tail)
    inputs = lax.all_to_all(outgoing, "space", split_axis=1, concat_axis=2, tiled=True)
    groups_here = window // group_width
    per_group = own_width // groups_here
    padding_one = ((1, 1), (1, 1), (1, 1))
    pre_two = lax.conv_general_dilated(
        inputs,
        weights_two,
        (1, 1, 1),
        padding_one,
        dimension_numbers=FIRST,
        feature_group_count=groups_here,
        preferred_element_type=jnp.float32,
    )
    axes_first = (0, 2, 3, 4)
    local_mean_two = jnp.mean(pre_two, axis=axes_first, keepdims=True)
    local_spread_two = jnp.sum(jnp.square(pre_two - local_mean_two), axis=axes_first, keepdims=True)
    local_count_two = float(pre_two.size // pre_two.shape[1])
    mean_two, spread_two, merged_two = butterfly_stats(
        local_mean_two, local_spread_two, local_count_two, ("dp",)
    )
    inv_two = lax.rsqrt(spread_two / merged_two + EPS)
    norm_two = (pre_two - mean_two) * inv_two
    gain_col = gain_two.reshape((1, -1, 1, 1, 1))
    shift_col = shift_two.reshape((1, -1, 1, 1, 1))
    result = (norm_two * gain_col + shift_col).astype(jnp.bfloat16)
    grad_norm_two = upstream.astype(jnp.float32) * gain_col * (1.0 / math.sqrt(count))
    first_sum, second_sum = _pair_sum(
        jnp.sum(grad_norm_two, axis=axes_first, keepdims=True),
        jnp.sum(grad_norm_two * norm_two, axis=axes_first, keepdims=True),
        ("dp",),
    )
    grad_pre_two = (
        inv_two * (grad_norm_two - first_sum / count - norm_two * (second_sum / count))
    ).astype(jnp.bfloat16)
    grouped_inputs = inputs.reshape((lead, groups_here, group_width) + inputs.shape[2:])
    grouped_grads = grad_pre_two.reshape((lead, groups_here, per_group) + grad_pre_two.shape[2:])
    pieces = jax.vmap(group_filter, in_axes=(1, 1))(grouped_inputs, grouped_grads)
    local_two = jnp.transpose(pieces, (1, 2, 3, 4, 0, 5)).reshape((3, 3, 3, group_width, own_width))
    flipped = weights_two[::-1, ::-1, ::-1]
    turned = (
        flipped.reshape((3, 3, 3, group_width, groups_here, per_group))
        .transpose((0, 1, 2, 5, 4, 3))
        .reshape((3, 3, 3, per_group, window))
    )
    partial_grad = lax.conv_general_dilated(
        grad_pre_two,
        turned,
        (1, 1, 1),
        padding_one,
        dimension_numbers=FIRST,
        feature_group_count=groups_here,
        preferred_element_type=jnp.float32,
    )
    arrived = lax.all_to_all(partial_grad, "space", split_axis=2, concat_axis=1, tiled=True)
    grad_act = jnp.sum(
        arrived.reshape((lead, channels // window, replicas, window) + arrived.shape[2:]), axis=2
    ).reshape((lead, channels) + arrived.shape[2:])
    grad_last = jnp.transpose(grad_act, (0, 2, 3, 4, 1))
    sigma = jax.nn.sigmoid(act_in)
    grad_norm_one = grad_last * (sigma * (1.0 + act_in * (1.0 - sigma))) * gain_one
    third_sum, fourth_sum = _pair_sum(
        jnp.sum(grad_norm_one, axis=axes_last),
        jnp.sum(grad_norm_one * norm_one, axis=axes_last),
        both,
    )
    grad_pre_one = (
        inv_one * (grad_norm_one - third_sum / count - norm_one * (fourth_sum / count))
    ).astype(jnp.bfloat16)
    gather_bits = 2
    group = 1 << gather_bits
    slab_size = stacked.size
    out_channels = grad_pre_one.shape[-1]
    width = out_channels // planes
    rows_one = grad_pre_one.shape[2:-1]
    ordered = jnp.moveaxis(
        grad_pre_one.reshape(rows_one + (planes // group, group, width)), -2, 0
    )
    packed = jnp.concatenate([stacked.reshape(-1), ordered.reshape(-1)])
    every = doubling_gather(packed, "space", gather_bits)
    slabs = every[:, :slab_size].reshape((group,) + stacked.shape[1:])
    combined = jnp.concatenate(
        [slabs[0, :1], slabs[:, 1:].reshape((-1,) + stacked.shape[2:])]
    )[None]
    grads = every[:, slab_size:].reshape((group, group) + rows_one + (out_channels // group,))
    rank = lax.axis_index("space") % group
    mine = lax.dynamic_index_in_dim(grads, rank, 1, False)[None]
    local_one = lax.conv_general_dilated(
        combined,
        mine,
        (1, 1, 1),
        ((0, 0), (1, 0), (1, 0)),
        rhs_dilation=(2, 2, 2),
        dimension_numbers=("CDHWN", "IDHWO", "CDHWN"),
        preferred_element_type=jnp.float32,
    )
    flat = local_one.reshape((planes // group, -1, 128))
    half = flat.shape[1] // 2
    chunk = jnp.concatenate(
        halving_scatter(
            (flat[:, :half], flat[:, half:]), "space", ((4, 2, 5, 3), (2, 4, 3, 5)), gather_bits
        )
    )
    chunk_shape = (width,) + local_one.shape[1:]
    joined = jnp.concatenate([chunk.reshape(-1), local_two.reshape(-1)])
    summed = butterfly_sum(joined, ("dp",))
    split = chunk.size
    grad_weights_one = jnp.transpose(summed[:split].reshape(chunk_shape), (1, 2, 3, 4, 0))
    grad_weights_two = summed[split:].reshape(local_two.shape)
    return (result, grad_weights_one, grad_weights_two)


def _pair_sum(first, second, axes):
    stacked = butterfly_sum(jnp.stack([first, second]), axes)
    return stacked[0], stacked[1]


def solution(mesh):
    return jax.shard_map(
        per_device,
        mesh=mesh,
        in_specs=(
            P("dp", "space", None, None, None),
            P(),
            P(),
            P(),
            P(None, None, None, None, "space"),
            P("space"),
            P("space"),
            P("dp", "space", None, None, None),
        ),
        out_specs=(
            P("dp", "space", None, None, None),
            P(None, None, None, None, "space"),
            P(None, None, None, None, "space"),
        ),
        check_vma=False,
    )
```
